256 devices in a mesh: row: 8 (over x, core), col: 32 (over y, z).
Axes of the slice: x: 4, y: 4, z: 8, core: 2. Of those that a mesh axis runs over, the one named last changes fastest.
Arguments:
- grid_points: int32 [2, 6, 4096], P(None, None, 'row'), may hold values from 0 to 127
- variable: int32 [6, 4096], P(None, 'row'), may hold values from 0 to 2
Outputs:
- panel_factor: float32 [6, 4096, 1536], P(None, ('row', 'col'))
- trailing: float32 [6, 4096, 16384], P(None, 'row', 'col')
The draws below stay inside these ranges and needn't reach their ends.
All inputs are finite; a program needn't handle non-finite values.
Results may differ from the reference program's by a relative error of at most 0.0042.
Values may be sent and summed in bfloat16 or wider, within the bound.
A program may use at most 128 MiB of HBM per device.

```python
import jax
import jax.numpy as jnp
from jax import lax

TILE = 512
PANELS = 3
GRID = 128
TILE_ROWS_DEV = 6
N_ROW = 8
N_COL = 32


def set_ends(array, own_key, least, top_value):
    shape = array.shape
    place = [jax.random.randint(jax.random.fold_in(own_key, axis), (), 0, shape[axis]) for axis in range(len(shape))]
    array = array.at[tuple(place)].set(least)
    longest = shape.index(max(shape))
    place[longest] = (place[longest] + 1) % shape[longest]
    return array.at[tuple(place)].set(top_value)


def setup_inputs(seed: int = 0) -> dict:
    streams_of = jax.random.split(jax.random.key(seed), 3)
    return {
        "grid_points": set_ends(jax.random.randint(streams_of[0], (2, TILE_ROWS_DEV, N_ROW * TILE), 0, GRID), jax.random.fold_in(streams_of[0], 1), 0, GRID - 1).astype(jnp.int32),
        "variable": set_ends(jax.random.randint(streams_of[1], (TILE_ROWS_DEV, N_ROW * TILE), 0, 3), jax.random.fold_in(streams_of[1], 1), 0, 2).astype(jnp.int32),
    }


range_scale = 0.05
nugget = 0.5
rho_first = 0.35
rho_second = 0.2
rho_third = 0.3
highest = lax.Precision.HIGHEST

def kind_scale(kinds):
    return jnp.where(kinds == 0, 1.0, jnp.where(kinds == 1, 1.3, 0.8))

def covariance(row_x, row_y, row_kind, col_x, col_y, col_kind):
    delta_x = (row_x[:, None] - col_x[None, :]).astype(jnp.float32)
    delta_y = (row_y[:, None] - col_y[None, :]).astype(jnp.float32)
    distance = jnp.sqrt(delta_x * delta_x + delta_y * delta_y) * (1.0 / (GRID * range_scale))
    order_sum = row_kind[:, None] + col_kind[None, :]
    dist_square = distance * distance
    dist_cube = dist_square * distance
    dist_fourth = dist_square * dist_square
    polynomial = jnp.where(order_sum == 0, 1.0, 1.0 + distance)
    polynomial = jnp.where(order_sum == 2, 1.0 + distance + dist_square / 3.0, polynomial)
    polynomial = jnp.where(order_sum == 3, 1.0 + distance + 0.4 * dist_square + dist_cube / 15.0, polynomial)
    polynomial = jnp.where(order_sum == 4, 1.0 + distance + dist_square * (3.0 / 7.0) + dist_cube * (2.0 / 21.0) + dist_fourth / 105.0, polynomial)
    correlation = jnp.where(row_kind[:, None] == col_kind[None, :], 1.0, jnp.where(order_sum == 1, rho_first, jnp.where(order_sum == 2, rho_second, rho_third)))
    scale_row = kind_scale(row_kind)
    scale_col = kind_scale(col_kind)
    return correlation * scale_row[:, None] * scale_col[None, :] * polynomial * jnp.exp(-distance)

def leading_factor(matrix, count, size):
    remaining = matrix
    lower_blocks = {}
    inverse_blocks = {}
    identity = jnp.eye(size, dtype=jnp.float32)
    for panel_step in range(count):
        row_begin = panel_step * size
        row_end = row_begin + size
        diag_factor = jnp.linalg.cholesky(remaining[row_begin:row_end, row_begin:row_end])
        diag_inverse = lax.linalg.triangular_solve(diag_factor, identity, left_side=True, lower=True)
        lower_blocks[panel_step, panel_step] = diag_factor
        inverse_blocks[panel_step, panel_step] = diag_inverse
        if panel_step + 1 < count:
            below_rows = jnp.dot(remaining[row_end:, row_begin:row_end], diag_inverse.T, precision=highest)
            for row_block in range(panel_step + 1, count):
                lower_blocks[row_block, panel_step] = below_rows[(row_block - panel_step - 1) * size:(row_block - panel_step) * size]
            trailing_part = remaining[row_end:, row_end:] - jnp.dot(below_rows, below_rows.T, precision=highest)
            remaining = remaining.at[row_end:, row_end:].set(trailing_part)
    for row_block in range(count):
        for col_block in range(row_block):
            running = jnp.zeros((size, size), jnp.float32)
            for mid_block in range(col_block, row_block):
                running = running + jnp.dot(lower_blocks[row_block, mid_block], inverse_blocks[mid_block, col_block], precision=highest)
            inverse_blocks[row_block, col_block] = -jnp.dot(inverse_blocks[row_block, row_block], running, precision=highest)
    zeros_block = jnp.zeros((size, size), jnp.float32)
    lower_rows = []
    inverse_rows = []
    for row_block in range(count):
        lower_rows.append(jnp.concatenate([lower_blocks[row_block, col_block] if col_block <= row_block else zeros_block for col_block in range(count)], 1))
        inverse_rows.append(jnp.concatenate([inverse_blocks[row_block, col_block] if col_block <= row_block else zeros_block for col_block in range(count)], 1))
    return (jnp.concatenate(lower_rows, 0), jnp.concatenate(inverse_rows, 0))

def reference(grid_points, variable):
    coord_x = grid_points[0].reshape(-1)
    coord_y = grid_points[1].reshape(-1)
    kinds = variable.reshape(-1)
    lead_size = PANELS * TILE
    order_all = coord_x.shape[0]
    lead_cov = covariance(coord_x[:lead_size], coord_y[:lead_size], kinds[:lead_size], coord_x[:lead_size], coord_y[:lead_size], kinds[:lead_size])
    lead_cov = lead_cov + nugget * jnp.eye(lead_size, dtype=jnp.float32)
    lower_factor, inverse = leading_factor(lead_cov, PANELS, TILE)
    rest_cov = covariance(coord_x[lead_size:], coord_y[lead_size:], kinds[lead_size:], coord_x[:lead_size], coord_y[:lead_size], kinds[:lead_size])
    solved = jnp.dot(rest_cov, inverse.T, precision=highest)
    panel_full = jnp.concatenate([lower_factor, solved], 0)
    panel_half = panel_full.astype(jnp.bfloat16)
    panel_wide = lax.optimization_barrier(panel_half).astype(jnp.float32)

    def column_tile(tile_index):
        col_start = lead_size + tile_index * TILE
        col_x = lax.dynamic_slice_in_dim(coord_x, col_start, TILE)
        col_y = lax.dynamic_slice_in_dim(coord_y, col_start, TILE)
        col_kind = lax.dynamic_slice_in_dim(kinds, col_start, TILE)
        cov_block = covariance(coord_x, coord_y, kinds, col_x, col_y, col_kind)
        equal = jnp.arange(order_all, dtype=jnp.int32)[:, None] == (col_start + jnp.arange(TILE, dtype=jnp.int32))[None, :]
        cov_block = jnp.where(equal, cov_block + nugget, cov_block)
        left_rows = lax.dynamic_slice_in_dim(panel_wide, col_start, TILE, 0)
        return cov_block - jnp.dot(panel_wide, left_rows.T, precision=highest)
    column_tiles = lax.map(column_tile, jnp.arange(N_COL, dtype=jnp.int32))
    trailing = jnp.transpose(column_tiles, (1, 0, 2)).reshape(order_all, N_COL * TILE)
    rows_dev = order_all // (N_ROW * TILE)
    return (panel_full.reshape(rows_dev, N_ROW * TILE, lead_size), trailing.reshape(rows_dev, N_ROW * TILE, N_COL * TILE))
```

```python
import functools, math
import jax, jax.numpy as jnp, numpy as np
from jax import lax
from jax.experimental import pallas as pl
from jax.experimental.pallas import tpu as pltpu
from jax.sharding import PartitionSpec as P
f32, bf16, i32 = jnp.float32, jnp.bfloat16, jnp.int32

TILE, LEAD, PANELS, SLOTS = 512, 1536, 3, 6
BLK, W = 128, 16
SCALE = 1.0 / (128 * 0.05)


def tables():
    bf = lambda z: np.asarray(z, np.float32).astype(bf16).astype(np.float32)
    forms = np.zeros((6, 16, 16), np.float32)
    forms[0, 0, 0] = forms[0, 1, 1] = -2.0
    forms[0, 2, 4] = forms[0, 4, 2] = 128.0
    forms[0, 3, 4] = forms[0, 5, 3] = 1.0
    sigma = (1.0, 1.3, 0.8)
    rho = {(0, 1): 0.35, (0, 2): 0.2, (1, 2): 0.3}
    shape = ((1,), (1, 1), (1, 1, 1 / 3), (1, 1, 2 / 5, 1 / 15), (1, 1, 3 / 7, 2 / 21, 1 / 105))
    for u in range(3):
        for w in range(3):
            base = (1.0 if u == w else rho[min(u, w), max(u, w)]) * sigma[u] * sigma[w]
            for d, a in enumerate(shape[u + w]):
                rest = base * a * SCALE**d
                for part in range(3):
                    top = float(bf(rest))
                    forms[1 + d, 6 + 3 * part + u, 6 + w] = top
                    rest -= top
    return forms.reshape(96, 16).astype(bf16)


def dot(a, b):
    return jnp.dot(a, b, preferred_element_type=f32)


def dot_nt(a, b):
    return lax.dot_general(a, b, (((1,), (1,)), ((), ())), preferred_element_type=f32)


def split(a):
    high = a.astype(bf16)
    return high, (a - high.astype(f32)).astype(bf16)


def features(ref):
    n = ref.shape[1]
    x, y, kind = ref[0:1, :], ref[1:2, :], ref[2:3, :]
    square = x * x + y * y
    row = lax.broadcasted_iota(i32, (16, n), 0)
    hot = jnp.where((row - 6) % 3 == kind, 1, 0)
    out = jnp.where(row >= 6, hot, 1)
    for index, value in enumerate((x, y, square >> 7, square & 127)):
        out = jnp.where(row == index, value, out)
    out = jnp.where(row == 15, 0, out)
    return out.astype(f32)


def cov(left, forms, cols):
    d2, c0, c1, c2, c3, c4 = (dot(left, forms[q, :, cols]) for q in range(6))
    t = d2 * lax.rsqrt(jnp.maximum(d2, 0.5))
    poly = (((c4 * t + c3) * t + c2) * t + c1) * t + c0
    return poly * jnp.exp2(t * (-SCALE * math.log2(math.e)))


def leaf(m_ref, n_ref):
    w = W
    row = lax.broadcasted_iota(i32, (w, BLK), 0)
    lane = lax.broadcasted_iota(i32, (w, BLK), 1)
    lane1 = lax.broadcasted_iota(i32, (1, BLK), 1)
    R = m_ref[0:w, :]
    n = BLK // w
    for s in range(n):
        K = w * s
        c = [jnp.broadcast_to(R[:, K + j:K + j + 1], (w, BLK)) for j in range(w)]
        inb = (lane >= K) & (lane < K + w)
        R = jnp.where(inb, jnp.where(lane - K == row, 1.0, 0.0), R)
        rr = jnp.zeros((w, BLK), f32)
        if s + 1 < n:
            old = m_ref[K + w:K + 2 * w, :]
            e = [jnp.broadcast_to(old[:, K + j:K + j + 1], (w, BLK)) for j in range(w)]
            nxt = jnp.where(inb, 0.0, old)
        for k in range(w):
            ck = c[k]
            r = lax.rsqrt(ck[k:k + 1, :])
            q = r * r
            Rk = R[k:k + 1, :]
            mk = jnp.where(row == k, 0.0, ck)
            n_ref[K + k:K + k + 1, :] = jnp.where(lane1 < K + w, Rk * r, 0.0)
            R = R - (mk * Rk) * q
            for j in range(k + 1, w):
                c[j] = c[j] - (mk * c[j][k:k + 1, :]) * q
            rr = jnp.where(row == k, q, rr)
        if s + 1 < n:
            T = R * rr
            acc = [None] * 4
            for j in range(w):
                v = e[j] * T[j:j + 1, :]
                acc[j % 4] = v if acc[j % 4] is None else acc[j % 4] + v
            R = nxt - ((acc[0] + acc[1]) + (acc[2] + acc[3]))
        if s + 2 < n:
            def emb(v):
                parts = [jnp.zeros((K, BLK), bf16)] if K else []
                parts += [v, jnp.zeros((BLK - K - w, BLK), bf16)]
                return jnp.concatenate(parts, 0)
            th, tl = (emb(v) for v in split(T))
            lane2 = lax.broadcasted_iota(i32, (BLK - K - 2 * w, BLK), 1)
            old = m_ref[K + 2 * w:, :]
            ah, al = split(old)
            upd = dot(ah, th) + dot(al, th) + dot(ah, tl)
            m_ref[K + 2 * w:, :] = jnp.where((lane2 >= K) & (lane2 < K + w), 0.0, old) - upd


def eye(n):
    return jnp.where(lax.broadcasted_iota(i32, (n, n), 0) == lax.broadcasted_iota(i32, (n, n), 1), 1.0, 0.0)


GC = 64


def main_kernel(where_ref, own_ref, lead_ref, target_ref, forms_ref, panel_ref, trail_ref,
                left, lead_forms, target_forms, g, vv, m_ref, n_ref, th, tl, ch, cl, pf, pj, ph, out, sems):
    row_index, col_index = where_ref[0], where_ref[1]
    forms = forms_ref[...]
    nl = LEAD
    for ref, dst, base in ((lead_ref, lead_forms, 3584), (target_ref, target_forms, 0), (own_ref, None, 512)):
        feat = features(ref)
        n = ref.shape[1]
        if dst is not None:
            all6 = dot(forms, feat.astype(bf16)).astype(bf16)
            for q in range(6):
                dst[q, :, :] = all6[16 * q:16 * q + 16, :]
        for b in range(0, n, 512):
            left[base + b:base + b + 512, :] = jnp.transpose(feat[:, b:b + 512]).astype(bf16)

    for ti in range(PANELS):
        def body(i, _, ti=ti):
            r0 = pl.multiple_of(ti * TILE + i * GC, GC)
            fl = left[pl.ds(3584 + r0, GC), :]
            for tj in range(2 * (ti + 1)):
                g[pl.ds(r0, GC), 256 * tj:256 * tj + 256] = cov(fl, lead_forms, slice(256 * tj, 256 * tj + 256))
            return 0
        lax.fori_loop(0, TILE // GC, body, 0)
    for k in range(LEAD // BLK):
        s = slice(BLK * k, BLK * k + BLK)
        g[s, s] = g[s, s] + 0.5 * eye(BLK)

    def step(k, _):
        k0 = pl.multiple_of(k * BLK, BLK)
        m_ref[...] = g[pl.ds(k0, BLK), pl.ds(k0, BLK)]
        leaf(m_ref, n_ref)
        dh, dl = split(n_ref[...])
        g[pl.ds(k0, BLK), :] = jnp.zeros((BLK, LEAD + BLK), f32)
        g[pl.ds(k0, BLK), pl.ds(k0, BLK)] = eye(BLK)
        def panel(i, _):
            r0 = pl.multiple_of(i * 512, 512)
            xh, xl = split(g[pl.ds(r0, 512), pl.ds(k0, BLK)])
            v = dot_nt(xh, dh) + dot_nt(xl, dh) + dot_nt(xh, dl)
            vh, vl = split(v)
            vv[pl.ds(r0, 512), 0:BLK] = vh
            vv[pl.ds(r0, 512), BLK:2 * BLK] = vl
            keep = lax.broadcasted_iota(i32, (512, BLK), 0) + r0 < k0 + BLK
            nh, nlo = split(jnp.where(keep, v, 0.0))
            th[pl.ds(r0, 512), pl.ds(k0, BLK)] = nh
            tl[pl.ds(r0, 512), pl.ds(k0, BLK)] = nlo
            return 0
        lax.fori_loop(0, 3, panel, 0)
        def update(j, _):
            c0 = pl.multiple_of(k0 + BLK + j * 256, BLK)
            lh = vv[pl.ds(c0, 256), 0:BLK]
            ll = vv[pl.ds(c0, 256), BLK:2 * BLK]
            l2 = jnp.concatenate([lh, lh], 1)
            def rows(i, _):
                r0 = pl.multiple_of(i * 512, 512)
                a = vv[pl.ds(r0, 512), :]
                upd = dot_nt(a, l2) + dot_nt(a[:, 0:BLK], ll)
                g[pl.ds(r0, 512), pl.ds(c0, 256)] = g[pl.ds(r0, 512), pl.ds(c0, 256)] - upd
                return 0
            lax.fori_loop(0, 3, rows, 0)
            return 0
        lax.fori_loop(0, (LEAD // BLK - k) // 2, update, 0)
        return 0
    lax.fori_loop(0, LEAD // BLK, step, 0)

    def tile(i, _):
        def gen(a, _):
            r0 = pl.multiple_of(a * GC, GC)
            fl = left[pl.ds(pl.multiple_of(i * TILE, TILE) + r0, GC), :]
            for tj in range(LEAD // 256):
                cols = slice(256 * tj, 256 * tj + 256)
                h, lo = split(cov(fl, lead_forms, cols))
                ch[pl.ds(r0, GC), cols] = h
                cl[pl.ds(r0, GC), cols] = lo
            return 0
        lax.fori_loop(0, TILE // GC, gen, 0)
        for q in range(PANELS):
            @pl.when((i == 1) & (row_index == q))
            def _():
                s = slice(TILE * q, TILE * q + TILE)
                h, lo = split(ch[:, s].astype(f32) + cl[:, s].astype(f32) + 0.5 * eye(TILE))
                ch[:, s] = h
                cl[:, s] = lo
        for u in range(LEAD // 256):
            depth = 256 * (u + 1)
            cols = slice(256 * u, depth)
            a, b = ch[:, 0:depth], cl[:, 0:depth]
            wh, wl = th[0:depth, cols], tl[0:depth, cols]
            pf[:, cols] = dot(a, wh) + dot(b, wh) + dot(a, wl)

        @pl.when(i == 0)
        def _():
            pj[...] = pf[...].astype(bf16)

        @pl.when(i > 0)
        def _():
            slot = lax.rem(i, 2)
            def store(n):
                return pltpu.make_async_copy(out.at[lax.rem(n, 2)], trail_ref.at[n - 1], sems.at[lax.rem(n, 2)])
            @pl.when(i > 2)
            def _():
                store(i - 2).wait()
            panel_ref[i - 1] = pf[pl.ds(pl.multiple_of(col_index * 16, 16), 16), :]
            ph[...] = pf[...].astype(bf16)
            def fin(a, _):
                r0 = pl.multiple_of(a * GC, GC)
                fl = left[pl.ds(pl.multiple_of(i * TILE, TILE) + r0, GC), :]
                for tj in range(TILE // 256):
                    cols = slice(256 * tj, 256 * tj + 256)
                    out[slot, pl.ds(r0, GC), cols] = cov(fl, target_forms, cols) - dot_nt(ph[pl.ds(r0, GC), :], pj[cols, :])
                return 0
            lax.fori_loop(0, TILE // GC, fin, 0)
            @pl.when((i - 1) * 8 + row_index == PANELS + col_index)
            def _():
                out[slot] = out[slot] + 0.5 * eye(TILE)
            store(i).start()
        return 0
    lax.fori_loop(0, SLOTS + 1, tile, 0)
    for n in (SLOTS - 1, SLOTS):
        pltpu.make_async_copy(out.at[n % 2], trail_ref.at[n - 1], sems.at[n % 2]).wait()


def main(where, own, lead, target, forms):
    vm = pl.BlockSpec(memory_space=pltpu.VMEM)
    scratch = [
        pltpu.VMEM((3584 + LEAD, 16), bf16),
        pltpu.VMEM((6, 16, LEAD), bf16),
        pltpu.VMEM((6, 16, TILE), bf16),
        pltpu.VMEM((LEAD, LEAD + BLK), f32),
        pltpu.VMEM((LEAD + BLK, 2 * BLK), bf16),
        pltpu.VMEM((BLK, BLK), f32),
        pltpu.VMEM((BLK, BLK), f32),
        pltpu.VMEM((LEAD, LEAD), bf16),
        pltpu.VMEM((LEAD, LEAD), bf16),
        pltpu.VMEM((TILE, LEAD), bf16),
        pltpu.VMEM((TILE, LEAD), bf16),
        pltpu.VMEM((TILE, LEAD), f32),
        pltpu.VMEM((TILE, LEAD), bf16),
        pltpu.VMEM((TILE, LEAD), bf16),
        pltpu.VMEM((2, TILE, TILE), f32),
        pltpu.SemaphoreType.DMA((2,)),
    ]
    return pl.pallas_call(
        main_kernel,
        out_shape=(jax.ShapeDtypeStruct((SLOTS, 16, LEAD), f32), jax.ShapeDtypeStruct((SLOTS, TILE, TILE), f32)),
        in_specs=[pl.BlockSpec(memory_space=pltpu.SMEM)] + [vm] * 4,
        out_specs=(vm, pl.BlockSpec(memory_space=pl.ANY)),
        scratch_shapes=scratch,
        compiler_params=pltpu.CompilerParams(vmem_limit_bytes=60 << 20),
        name="panels",
    )(where, own, lead, target, forms)


def local(grid_points, variable):
    row_index, col_index = lax.axis_index("row"), lax.axis_index("col")
    mine = jnp.concatenate([grid_points, variable[None], jnp.zeros((5,) + variable.shape, i32)], 0)
    both = jnp.moveaxis(mine[:3], 1, 0)
    everyone = lax.all_gather(both, "row", axis=1, tiled=False)
    everyone = everyone.reshape(-1, 3, TILE)
    pad = lambda z: jnp.concatenate([z, jnp.zeros((8 - z.shape[0], z.shape[1]), i32)], 0)
    lead = pad(jnp.moveaxis(everyone[:PANELS], 1, 0).reshape(3, LEAD))
    target = pad(lax.dynamic_index_in_dim(everyone, PANELS + col_index, 0, False))
    where = jnp.stack([row_index, col_index]).astype(i32)
    return main(where, mine.reshape(8, SLOTS * TILE), lead, target, jnp.asarray(tables()))


def solution(mesh):
    return jax.shard_map(
        local,
        mesh=mesh,
        in_specs=(P(None, None, "row"), P(None, "row")),
        out_specs=(P(None, ("row", "col"), None), P(None, "row", "col")),
        check_vma=False,
    )
```

```python
import functools, math
import jax, jax.numpy as jnp, numpy as np
from jax import lax
from jax.experimental import pallas as pl
from jax.experimental.pallas import tpu as pltpu
from jax.sharding import PartitionSpec as P
f32, bf16, i32 = jnp.float32, jnp.bfloat16, jnp.int32

TILE, LEAD, PANELS, SLOTS = 512, 1536, 3, 6
BLK, W = 128, 16
SCALE = 1.0 / (128 * 0.05)


def tables():
    bf = lambda z: np.asarray(z, np.float32).astype(bf16).astype(np.float32)
    forms = np.zeros((6, 16, 16), np.float32)
    forms[0, 0, 0] = forms[0, 1, 1] = -2.0
    forms[0, 2, 4] = forms[0, 4, 2] = 128.0
    forms[0, 3, 4] = forms[0, 5, 3] = 1.0
    sigma = (1.0, 1.3, 0.8)
    rho = {(0, 1): 0.35, (0, 2): 0.2, (1, 2): 0.3}
    shape = ((1,), (1, 1), (1, 1, 1 / 3), (1, 1, 2 / 5, 1 / 15), (1, 1, 3 / 7, 2 / 21, 1 / 105))
    for u in range(3):
        for w in range(3):
            base = (1.0 if u == w else rho[min(u, w), max(u, w)]) * sigma[u] * sigma[w]
            for d, a in enumerate(shape[u + w]):
                rest = base * a * SCALE**d
                for part in range(3):
                    top = float(bf(rest))
                    forms[1 + d, 6 + 3 * part + u, 6 + w] = top
                    rest -= top
    return forms.reshape(96, 16).astype(bf16)


def dot(a, b):
    return jnp.dot(a, b, preferred_element_type=f32)


def dot_nt(a, b):
    return lax.dot_general(a, b, (((1,), (1,)), ((), ())), preferred_element_type=f32)


def split(a):
    high = a.astype(bf16)
    return high, (a - high.astype(f32)).astype(bf16)


def features(x, y, kind):
    n = x.shape[1]
    square = x * x + y * y
    row = lax.broadcasted_iota(i32, (16, n), 0)
    hot = jnp.where((row - 6) % 3 == kind, 1, 0)
    out = jnp.where(row >= 6, hot, 1)
    for index, value in enumerate((x, y, square >> 7, square & 127)):
        out = jnp.where(row == index, value, out)
    out = jnp.where(row == 15, 0, out)
    return out.astype(f32)


def cov(left, forms, cols):
    d2, c0, c1, c2, c3, c4 = (dot(left, forms[q, :, cols]) for q in range(6))
    t = d2 * lax.rsqrt(jnp.maximum(d2, 0.5))
    poly = (((c4 * t + c3) * t + c2) * t + c1) * t + c0
    return poly * jnp.exp2(t * (-SCALE * math.log2(math.e)))


def leaf(m_ref, n_ref, fill=lambda at: None):
    w = W
    row = lax.broadcasted_iota(i32, (w, BLK), 0)
    lane = lax.broadcasted_iota(i32, (w, BLK), 1)
    lane1 = lax.broadcasted_iota(i32, (1, BLK), 1)
    R = m_ref[0:w, :]
    n = BLK // w
    for s in range(n):
        K = w * s
        c = [jnp.broadcast_to(R[:, K + j:K + j + 1], (w, BLK)) for j in range(w)]
        inb = (lane >= K) & (lane < K + w)
        R = jnp.where(inb, jnp.where(lane - K == row, 1.0, 0.0), R)
        rr = jnp.zeros((w, BLK), f32)
        if s + 1 < n:
            old = m_ref[K + w:K + 2 * w, :]
            e = [jnp.broadcast_to(old[:, K + j:K + j + 1], (w, BLK)) for j in range(w)]
            nxt = jnp.where(inb, 0.0, old)
        for k in range(w):
            ck = c[k]
            r = lax.rsqrt(ck[k:k + 1, :])
            q = r * r
            Rk = R[k:k + 1, :]
            mk = jnp.where(row == k, 0.0, ck)
            n_ref[K + k:K + k + 1, :] = jnp.where(lane1 < K + w, Rk * r, 0.0)
            R = R - (mk * Rk) * q
            for j in range(k + 1, w):
                c[j] = c[j] - (mk * c[j][k:k + 1, :]) * q
            rr = jnp.where(row == k, q, rr)
            fill(K + k)
        if s + 1 < n:
            T = R * rr
            acc = [None] * 4
            for j in range(w):
                v = e[j] * T[j:j + 1, :]
                acc[j % 4] = v if acc[j % 4] is None else acc[j % 4] + v
            R = nxt - ((acc[0] + acc[1]) + (acc[2] + acc[3]))
        if s + 2 < n:
            def emb(v):
                parts = [jnp.zeros((K, BLK), bf16)] if K else []
                parts += [v, jnp.zeros((BLK - K - w, BLK), bf16)]
                return jnp.concatenate(parts, 0)
            th, tl = (emb(v) for v in split(T))
            lane2 = lax.broadcasted_iota(i32, (BLK - K - 2 * w, BLK), 1)
            old = m_ref[K + 2 * w:, :]
            ah, al = split(old)
            upd = dot(ah, th) + dot(al, th) + dot(ah, tl)
            m_ref[K + 2 * w:, :] = jnp.where((lane2 >= K) & (lane2 < K + w), 0.0, old) - upd


def eye(n):
    return jnp.where(lax.broadcasted_iota(i32, (n, n), 0) == lax.broadcasted_iota(i32, (n, n), 1), 1.0, 0.0)


RB = 4
PB = 384
U1, U2, U3 = 8, 7, 8


def main_kernel(points_ref, kinds_ref, sites_ref, forms_ref, panel_ref, trail_ref,
                left, lead_forms, target_forms, g, vv, m_ref, n_ref, dd, th, tl, ch, cl, pf, pj, ph, out, sems):
    row_index, col_index = lax.axis_index("row"), lax.axis_index("col")
    forms = forms_ref[...]
    def prepare(x, y, kind, base, dst, at):
        feat = features(x, y, kind)
        n = feat.shape[1]
        left[base:base + n, :] = jnp.transpose(feat).astype(bf16)
        if dst is not None:
            all6 = dot(forms, feat.astype(bf16)).astype(bf16)
            for q in range(6):
                dst[q, :, at:at + n] = all6[16 * q:16 * q + 16, :]
    for q in range(PANELS):
        prepare(*(sites_ref[q, d:d + 1, :] for d in range(3)), 3584 + TILE * q, lead_forms, TILE * q)
    owner = lax.rem(col_index + PANELS, sites_ref.shape[0])
    prepare(*(sites_ref[owner, d:d + 1, :] for d in range(3, 6)), 0, target_forms, 0)
    for q in range(SLOTS):
        prepare(points_ref[0, q:q + 1, :], points_ref[1, q:q + 1, :], kinds_ref[q:q + 1, :], 512 + TILE * q, None, 0)

    def lead_unit(ti, tj):
        rows, cols = slice(256 * ti, 256 * ti + 256), slice(256 * tj, 256 * tj + 256)
        block = cov(left[3584 + 256 * ti:3840 + 256 * ti, :], lead_forms, cols)
        g[rows, cols] = block + 0.5 * eye(256) if ti == tj else block

    def own_unit(n):
        r0 = pl.multiple_of(n // 6 * 256, 256)
        c0 = pl.multiple_of(lax.rem(n, 6) * 256, 256)
        h, lo = split(cov(left[pl.ds(r0, 256), :], lead_forms, pl.ds(c0, 256)))
        ch[pl.ds(r0, 256), pl.ds(c0, 256)] = h
        cl[pl.ds(r0, 256), pl.ds(c0, 256)] = lo

    def panel(p0, i):
        rows = slice(PB * i, PB * i + PB)
        xh, xl = split(g[rows, pl.ds(p0, BLK)])
        v = dot_nt(jnp.concatenate([xh, xl], 1), dd[:, 0:2 * BLK]) + dot_nt(xh, dd[:, 2 * BLK:])
        vh, vl = split(v)
        vv[rows, 0:BLK] = vh
        vv[rows, BLK:2 * BLK] = vl
        keep = lax.broadcasted_iota(i32, (PB, BLK), 0) + PB * i < p0 + BLK
        th[rows, pl.ds(p0, BLK)] = jnp.where(keep, vh, jnp.zeros_like(vh))
        tl[rows, pl.ds(p0, BLK)] = jnp.where(keep, vl, jnp.zeros_like(vl))

    def update(k0, j, blocks):
        c0 = k0 + j * 256
        cols = pl.ds(pl.multiple_of(jnp.minimum(c0, LEAD), BLK), 256)
        rows = [pl.ds(pl.multiple_of(lax.rem(c0 + n * BLK, LEAD), BLK), BLK) for n in blocks]
        lh, ll = vv[cols, 0:BLK], vv[cols, BLK:2 * BLK]
        a = jnp.concatenate([vv[r, :] for r in rows], 0)
        upd = dot_nt(a, jnp.concatenate([lh, lh], 1)) + dot_nt(a[:, 0:BLK], ll)
        for n, r in enumerate(rows):
            g[r, cols] = g[r, cols] - upd[n * BLK:n * BLK + BLK, :]

    lead_unit(0, 0)
    vv[LEAD:, :] = jnp.zeros((2 * BLK, 2 * BLK), bf16)
    m_ref[...] = g[0:BLK, 0:BLK]

    def step(slots, units, base, k, _):
        k0 = pl.multiple_of(k * BLK, BLK)
        p0 = pl.multiple_of(k * BLK - BLK, BLK)
        if slots:
            work = [functools.partial(panel, p0, i) for i in range(LEAD // PB)]
            bulk = [functools.partial(update, k0, j, range(n, min(n + RB, 12 - 2 * j))) for j in range(slots) for n in range(0, 12 - 2 * j, RB)]
            own = [lambda n=n: own_unit(k * units + base + n) for n in range(units)]
            mix = sorted([((n + 0.5) / len(bulk), f) for n, f in enumerate(bulk)] + [((n + 0.5) / len(own), f) for n, f in enumerate(own)], key=lambda z: z[0])
            work += [f for _, f in mix]
        else:
            work = [functools.partial(lead_unit, ti, tj) for ti in range(6) for tj in range(ti + 1) if ti]
        def fill(at):
            for n in range(at * len(work) // BLK, (at + 1) * len(work) // BLK):
                work[n]()
        leaf(m_ref, n_ref, fill)
        dh, dl = split(n_ref[...])
        dd[:, 0:BLK] = dh
        dd[:, BLK:2 * BLK] = dh
        dd[:, 2 * BLK:] = dl
        k1 = pl.multiple_of(jnp.minimum(k0 + BLK, LEAD - BLK), BLK)
        xh, xl = split(g[pl.ds(k1, BLK), pl.ds(k0, BLK)])
        h, lo = split(dot_nt(xh, dh) + dot_nt(xl, dh) + dot_nt(xh, dl))
        m_ref[...] = g[pl.ds(k1, BLK), pl.ds(k1, BLK)] - (dot_nt(h, h) + dot_nt(lo, h) + dot_nt(h, lo))
        g[pl.ds(k0, BLK), :] = jnp.zeros((BLK, LEAD + 2 * BLK), f32)
        g[pl.ds(k0, BLK), pl.ds(k0, BLK)] = eye(BLK)
        return 0
    step(0, 0, 0, 0, 0)
    lax.fori_loop(1, 4, functools.partial(step, 6, U1, -U1), 0)
    lax.fori_loop(4, 8, functools.partial(step, 4, U2, 3 * U1 - 4 * U2), 0)
    lax.fori_loop(8, 12, functools.partial(step, 2, U3, 3 * U1 + 4 * U2 - 8 * U3), 0)
    for i in range(LEAD // PB):
        panel(LEAD - BLK, i)

    def tile(i, _):
        t0 = pl.multiple_of(i * TILE, TILE)
        rows = pl.ds(t0, TILE)
        for q in range(PANELS):
            @pl.when((i == 1) & (row_index == q))
            def _():
                s = slice(TILE * q, TILE * q + TILE)
                h, lo = split(ch[rows, s].astype(f32) + cl[rows, s].astype(f32) + 0.5 * eye(TILE))
                ch[rows, s] = h
                cl[rows, s] = lo
        slot = lax.rem(i, 2)
        def store(n):
            return pltpu.make_async_copy(out.at[lax.rem(n, 2)], trail_ref.at[n - 1], sems.at[lax.rem(n, 2)])
        @pl.when(i > 2)
        def _():
            store(i - 2).wait()
        spot = pl.multiple_of(col_index * 16, 16)
        for u in range(LEAD // 256):
            depth = 256 * (u + 1)
            cols = slice(256 * u, depth)
            a, b = ch[rows, 0:depth], cl[rows, 0:depth]
            wh, wl = th[0:depth, cols], tl[0:depth, cols]
            pf[...] = dot(a, wh) + dot(b, wh) + dot(a, wl)
            panel_ref[jnp.maximum(i - 1, 0), :, cols] = pf[pl.ds(spot, 16), :]
            ph[:, cols] = pf[...].astype(bf16)
            if u >= 2:
                rr, cc = (u - 2) // 2 * 256, (u - 2) % 2 * 256
                fl = left[pl.ds(t0 + rr, 256), :]
                out[slot, rr:rr + 256, cc:cc + 256] = cov(fl, target_forms, slice(cc, cc + 256))

        @pl.when(i == 0)
        def _():
            pj[...] = ph[...]

        @pl.when(i > 0)
        def _():
            for tj in range(TILE // 256):
                cols = slice(256 * tj, 256 * tj + 256)
                out[slot, :, cols] = out[slot, :, cols] - dot_nt(ph[...], pj[cols, :])
            @pl.when((i - 1) * 8 + row_index == PANELS + col_index)
            def _():
                out[slot] = out[slot] + 0.5 * eye(TILE)
            store(i).start()
        return 0
    lax.fori_loop(0, SLOTS + 1, tile, 0)
    for n in (SLOTS - 1, SLOTS):
        pltpu.make_async_copy(out.at[n % 2], trail_ref.at[n - 1], sems.at[n % 2]).wait()


def exchange_kernel(send_ref, o_ref, buf, send_sem, recv_sem):
    me = lax.axis_index("row")
    count = buf.shape[0]
    other = lambda d: {"row": lax.rem(me + d, count)}
    barrier = pltpu.get_barrier_semaphore()
    for d in range(1, count):
        pl.semaphore_signal(barrier, inc=1, device_id=other(d), device_id_type=pl.DeviceIdType.MESH)
    pl.semaphore_wait(barrier, count - 1)

    def copy(d, place):
        return pltpu.make_async_remote_copy(
            src_ref=send_ref, dst_ref=buf.at[place], send_sem=send_sem.at[d - 1], recv_sem=recv_sem.at[d - 1],
            device_id=other(d), device_id_type=pl.DeviceIdType.MESH)
    for d in range(1, count):
        copy(d, me).start()
    buf[me] = send_ref[...]
    for d in range(1, count):
        copy(d, lax.rem(me + count - d, count)).wait_recv()
    for d in range(1, count):
        copy(d, me).wait_send()
    o_ref[...] = buf[...]


def exchange(send, count):
    vm = pl.BlockSpec(memory_space=pltpu.VMEM)
    shape = (count,) + send.shape
    return pl.pallas_call(
        exchange_kernel,
        out_shape=jax.ShapeDtypeStruct(shape, send.dtype),
        in_specs=[vm],
        out_specs=vm,
        scratch_shapes=[pltpu.VMEM(shape, send.dtype), pltpu.SemaphoreType.DMA((count - 1,)), pltpu.SemaphoreType.DMA((count - 1,))],
        compiler_params=pltpu.CompilerParams(collective_id=0, has_side_effects=True),
        name="exchange",
    )(send)


def main(points, kinds, sites, forms):
    vm = pl.BlockSpec(memory_space=pltpu.VMEM)
    scratch = [
        pltpu.VMEM((3584 + LEAD, 16), bf16),
        pltpu.VMEM((6, 16, LEAD), bf16),
        pltpu.VMEM((6, 16, TILE), bf16),
        pltpu.VMEM((LEAD, LEAD + 2 * BLK), f32),
        pltpu.VMEM((LEAD + 2 * BLK, 2 * BLK), bf16),
        pltpu.VMEM((BLK, BLK), f32),
        pltpu.VMEM((BLK, BLK), f32),
        pltpu.VMEM((BLK, 3 * BLK), bf16),
        pltpu.VMEM((LEAD, LEAD), bf16),
        pltpu.VMEM((LEAD, LEAD), bf16),
        pltpu.VMEM((7 * TILE, LEAD), bf16),
        pltpu.VMEM((7 * TILE, LEAD), bf16),
        pltpu.VMEM((TILE, 256), f32),
        pltpu.VMEM((TILE, LEAD), bf16),
        pltpu.VMEM((TILE, LEAD), bf16),
        pltpu.VMEM((2, TILE, TILE), f32),
        pltpu.SemaphoreType.DMA((2,)),
    ]
    return pl.pallas_call(
        main_kernel,
        out_shape=(jax.ShapeDtypeStruct((SLOTS, 16, LEAD), f32), jax.ShapeDtypeStruct((SLOTS, TILE, TILE), f32)),
        in_specs=[vm] * 4,
        out_specs=(vm, pl.BlockSpec(memory_space=pl.ANY)),
        scratch_shapes=scratch,
        compiler_params=pltpu.CompilerParams(vmem_limit_bytes=60 << 20),
        name="panels",
    )(points, kinds, sites, forms)


def local(grid_points, variable):
    count = lax.axis_size("row")
    place = (PANELS + lax.axis_index("col")) // count
    second = lax.dynamic_index_in_dim(grid_points, place, 1, False)
    kind = lax.dynamic_index_in_dim(variable, place, 0, True)
    send = jnp.concatenate([grid_points[:, 0], variable[:1], second, kind, jnp.zeros((2, TILE), i32)], 0)
    return main(grid_points, variable, exchange(send, count), jnp.asarray(tables()))


def solution(mesh):
    return jax.shard_map(
        local,
        mesh=mesh,
        in_specs=(P(None, None, "row"), P(None, "row")),
        out_specs=(P(None, ("row", "col"), None), P(None, "row", "col")),
        check_vma=False,
    )
```

```python
import functools, math
import jax, jax.numpy as jnp, numpy as np
from jax import lax
from jax.experimental import pallas as pl
from jax.experimental.pallas import tpu as pltpu
from jax.sharding import PartitionSpec as P
f32, bf16, i32 = jnp.float32, jnp.bfloat16, jnp.int32

TILE, LEAD, PANELS, SLOTS = 512, 1536, 3, 6
BLK, W = 128, 16
SCALE = 1.0 / (128 * 0.05)


def tables():
    bf = lambda z: np.asarray(z, np.float32).astype(bf16).astype(np.float32)
    forms = np.zeros((6, 16, 16), np.float32)
    forms[0, 0, 0] = forms[0, 1, 1] = -2.0
    forms[0, 2, 4] = forms[0, 4, 2] = 128.0
    forms[0, 3, 4] = forms[0, 5, 3] = 1.0
    sigma = (1.0, 1.3, 0.8)
    rho = {(0, 1): 0.35, (0, 2): 0.2, (1, 2): 0.3}
    shape = ((1,), (1, 1), (1, 1, 1 / 3), (1, 1, 2 / 5, 1 / 15), (1, 1, 3 / 7, 2 / 21, 1 / 105))
    for u in range(3):
        for w in range(3):
            base = (1.0 if u == w else rho[min(u, w), max(u, w)]) * sigma[u] * sigma[w]
            for d, a in enumerate(shape[u + w]):
                rest = base * a * SCALE**d
                for part in range(3):
                    top = float(bf(rest))
                    forms[1 + d, 6 + 3 * part + u, 6 + w] = top
                    rest -= top
    return forms.reshape(96, 16).astype(bf16)


def dot(a, b):
    return jnp.dot(a, b, preferred_element_type=f32)


def dot_nt(a, b):
    return lax.dot_general(a, b, (((1,), (1,)), ((), ())), preferred_element_type=f32)


def split(a):
    high = a.astype(bf16)
    return high, (a - high.astype(f32)).astype(bf16)


def features(x, y, kind):
    n = x.shape[1]
    square = x * x + y * y
    row = lax.broadcasted_iota(i32, (16, n), 0)
    hot = jnp.where((row - 6) % 3 == kind, 1, 0)
    out = jnp.where(row >= 6, hot, 1)
    for index, value in enumerate((x, y, square >> 7, square & 127)):
        out = jnp.where(row == index, value, out)
    out = jnp.where(row == 15, 0, out)
    return out.astype(f32)


def cov(left, forms, cols):
    d2, c0, c1, c2, c3, c4 = (dot(left, forms[q, :, cols]) for q in range(6))
    t = d2 * lax.rsqrt(jnp.maximum(d2, 0.5))
    poly = (((c4 * t + c3) * t + c2) * t + c1) * t + c0
    return poly * jnp.exp2(t * (-SCALE * math.log2(math.e)))


def leaf(m_ref, n_ref, fill=lambda at: None):
    w = W
    row = lax.broadcasted_iota(i32, (w, BLK), 0)
    lane = lax.broadcasted_iota(i32, (w, BLK), 1)
    lane1 = lax.broadcasted_iota(i32, (1, BLK), 1)
    R = m_ref[0:w, :]
    n = BLK // w
    for s in range(n):
        K = w * s
        c = [jnp.broadcast_to(R[:, K + j:K + j + 1], (w, BLK)) for j in range(w)]
        inb = (lane >= K) & (lane < K + w)
        R = jnp.where(inb, jnp.where(lane - K == row, 1.0, 0.0), R)
        rr = jnp.zeros((w, BLK), f32)
        if s + 1 < n:
            old = m_ref[K + w:K + 2 * w, :]
            e = [jnp.broadcast_to(old[:, K + j:K + j + 1], (w, BLK)) for j in range(w)]
            nxt = jnp.where(inb, 0.0, old)
        for k in range(w):
            ck = c[k]
            r = lax.rsqrt(ck[k:k + 1, :])
            q = r * r
            Rk = R[k:k + 1, :]
            mk = jnp.where(row == k, 0.0, ck)
            n_ref[K + k:K + k + 1, :] = jnp.where(lane1 < K + w, Rk * r, 0.0)
            R = R - (mk * Rk) * q
            for j in range(k + 1, w):
                c[j] = c[j] - (mk * c[j][k:k + 1, :]) * q
            rr = jnp.where(row == k, q, rr)
            fill(K + k)
        if s + 1 < n:
            T = R * rr
            acc = [None] * 4
            for j in range(w):
                v = e[j] * T[j:j + 1, :]
                acc[j % 4] = v if acc[j % 4] is None else acc[j % 4] + v
            R = nxt - ((acc[0] + acc[1]) + (acc[2] + acc[3]))
        if s + 2 < n:
            def emb(v):
                parts = [jnp.zeros((K, BLK), bf16)] if K else []
                parts += [v, jnp.zeros((BLK - K - w, BLK), bf16)]
                return jnp.concatenate(parts, 0)
            th, tl = (emb(v) for v in split(T))
            lane2 = lax.broadcasted_iota(i32, (BLK - K - 2 * w, BLK), 1)
            old = m_ref[K + 2 * w:, :]
            ah, al = split(old)
            upd = dot(ah, th) + dot(al, th) + dot(ah, tl)
            m_ref[K + 2 * w:, :] = jnp.where((lane2 >= K) & (lane2 < K + w), 0.0, old) - upd


def eye(n):
    return jnp.where(lax.broadcasted_iota(i32, (n, n), 0) == lax.broadcasted_iota(i32, (n, n), 1), 1.0, 0.0)


RB = 4
PB = 384
U1, U2, U3 = 8, 7, 8


def main_kernel(points_ref, kinds_ref, sites_ref, forms_ref, panel_ref, trail_ref,
                left, lead_forms, target_forms, g, vv, m_ref, n_ref, dd, th, tl, ch, cl, pf, pj, ph, out, sems):
    row_index, col_index = lax.axis_index("row"), lax.axis_index("col")
    forms = forms_ref[...]
    def prepare(x, y, kind, base, dst, at):
        feat = features(x, y, kind)
        n = feat.shape[1]
        left[base:base + n, :] = jnp.transpose(feat).astype(bf16)
        if dst is not None:
            all6 = dot(forms, feat.astype(bf16)).astype(bf16)
            for q in range(6):
                dst[q, :, at:at + n] = all6[16 * q:16 * q + 16, :]
    for q in range(PANELS):
        prepare(*(sites_ref[q, d:d + 1, :] for d in range(3)), 3584 + TILE * q, lead_forms, TILE * q)
    owner = lax.rem(col_index + PANELS, sites_ref.shape[0])
    prepare(*(sites_ref[owner, d:d + 1, :] for d in range(3, 6)), 0, target_forms, 0)
    for q in range(SLOTS):
        prepare(points_ref[0, q:q + 1, :], points_ref[1, q:q + 1, :], kinds_ref[q:q + 1, :], 512 + TILE * q, None, 0)

    def lead_unit(ti, tj):
        rows, cols = slice(256 * ti, 256 * ti + 256), slice(256 * tj, 256 * tj + 256)
        block = cov(left[3584 + 256 * ti:3840 + 256 * ti, :], lead_forms, cols)
        g[rows, cols] = block + 0.5 * eye(256) if ti == tj else block

    def own_unit(n):
        r0 = pl.multiple_of(n // 6 * 256, 256)
        c0 = pl.multiple_of(lax.rem(n, 6) * 256, 256)
        h, lo = split(cov(left[pl.ds(r0, 256), :], lead_forms, pl.ds(c0, 256)))
        ch[pl.ds(r0, 256), pl.ds(c0, 256)] = h
        cl[pl.ds(r0, 256), pl.ds(c0, 256)] = lo

    def panel(p0, i):
        rows = slice(PB * i, PB * i + PB)
        xh, xl = split(g[rows, pl.ds(p0, BLK)])
        v = dot_nt(jnp.concatenate([xh, xl], 1), dd[:, 0:2 * BLK]) + dot_nt(xh, dd[:, 2 * BLK:])
        vh, vl = split(v)
        vv[rows, 0:BLK] = vh
        vv[rows, BLK:2 * BLK] = vl
        keep = lax.broadcasted_iota(i32, (PB, BLK), 0) + PB * i < p0 + BLK
        th[rows, pl.ds(p0, BLK)] = jnp.where(keep, vh, jnp.zeros_like(vh))
        tl[rows, pl.ds(p0, BLK)] = jnp.where(keep, vl, jnp.zeros_like(vl))

    def update(k0, j, blocks):
        c0 = k0 + j * 256
        cols = pl.ds(pl.multiple_of(jnp.minimum(c0, LEAD), BLK), 256)
        rows = [pl.ds(pl.multiple_of(lax.rem(c0 + n * BLK, LEAD), BLK), BLK) for n in blocks]
        lh, ll = vv[cols, 0:BLK], vv[cols, BLK:2 * BLK]
        a = jnp.concatenate([vv[r, :] for r in rows], 0)
        upd = dot_nt(a, jnp.concatenate([lh, lh], 1)) + dot_nt(a[:, 0:BLK], ll)
        for n, r in enumerate(rows):
            g[r, cols] = g[r, cols] - upd[n * BLK:n * BLK + BLK, :]

    lead_unit(0, 0)
    vv[LEAD:, :] = jnp.zeros((2 * BLK, 2 * BLK), bf16)
    m_ref[...] = g[0:BLK, 0:BLK]

    def step(slots, units, base, k, _):
        k0 = pl.multiple_of(k * BLK, BLK)
        p0 = pl.multiple_of(k * BLK - BLK, BLK)
        if slots:
            work = [functools.partial(panel, p0, i) for i in range(LEAD // PB)]
            bulk = [functools.partial(update, k0, j, range(n, min(n + RB, 12 - 2 * j))) for j in range(slots) for n in range(0, 12 - 2 * j, RB)]
            own = [lambda n=n: own_unit(k * units + base + n) for n in range(units)]
            mix = sorted([((n + 0.5) / len(bulk), f) for n, f in enumerate(bulk)] + [((n + 0.5) / len(own), f) for n, f in enumerate(own)], key=lambda z: z[0])
            work += [f for _, f in mix]
        else:
            work = [functools.partial(lead_unit, ti, tj) for ti in range(6) for tj in range(ti + 1) if ti]
        def fill(at):
            for n in range(at * len(work) // BLK, (at + 1) * len(work) // BLK):
                work[n]()
        leaf(m_ref, n_ref, fill)
        dh, dl = split(n_ref[...])
        dd[:, 0:BLK] = dh
        dd[:, BLK:2 * BLK] = dh
        dd[:, 2 * BLK:] = dl
        k1 = pl.multiple_of(jnp.minimum(k0 + BLK, LEAD - BLK), BLK)
        xh, xl = split(g[pl.ds(k1, BLK), pl.ds(k0, BLK)])
        h, lo = split(dot_nt(xh, dh) + dot_nt(xl, dh) + dot_nt(xh, dl))
        m_ref[...] = g[pl.ds(k1, BLK), pl.ds(k1, BLK)] - (dot_nt(h, h) + dot_nt(lo, h) + dot_nt(h, lo))
        g[pl.ds(k0, BLK), :] = jnp.zeros((BLK, LEAD + 2 * BLK), f32)
        g[pl.ds(k0, BLK), pl.ds(k0, BLK)] = eye(BLK)
        return 0
    step(0, 0, 0, 0, 0)
    lax.fori_loop(1, 4, functools.partial(step, 6, U1, -U1), 0)
    lax.fori_loop(4, 8, functools.partial(step, 4, U2, 3 * U1 - 4 * U2), 0)
    lax.fori_loop(8, 12, functools.partial(step, 2, U3, 3 * U1 + 4 * U2 - 8 * U3), 0)
    for i in range(LEAD // PB):
        panel(LEAD - BLK, i)

    def tile(i, _):
        t0 = pl.multiple_of(i * TILE, TILE)
        rows = pl.ds(t0, TILE)
        for q in range(PANELS):
            @pl.when((i == 1) & (row_index == q))
            def _():
                s = slice(TILE * q, TILE * q + TILE)
                h, lo = split(ch[rows, s].astype(f32) + cl[rows, s].astype(f32) + 0.5 * eye(TILE))
                ch[rows, s] = h
                cl[rows, s] = lo
        slot = lax.rem(i, 2)
        def store(n):
            return pltpu.make_async_copy(out.at[lax.rem(n, 2)], trail_ref.at[n - 1], sems.at[lax.rem(n, 2)])
        @pl.when(i > 2)
        def _():
            store(i - 2).wait()
        spot = pl.multiple_of(col_index * 16, 16)
        for u in range(LEAD // 256):
            depth = 256 * (u + 1)
            cols = slice(256 * u, depth)
            a, b = ch[rows, 0:depth], cl[rows, 0:depth]
            wh, wl = th[0:depth, cols], tl[0:depth, cols]
            pf[...] = dot(a, wh) + dot(b, wh) + dot(a, wl)
            panel_ref[jnp.maximum(i - 1, 0), :, cols] = pf[pl.ds(spot, 16), :]
            ph[:, cols] = pf[...].astype(bf16)

        @pl.when(i == 0)
        def _():
            pj[...] = ph[...]

        @pl.when(i > 0)
        def _():
            for rr, cc in ((0, 0), (0, 256), (256, 0), (256, 256)):
                fl = left[pl.ds(t0 + rr, 256), :]
                out[slot, rr:rr + 256, cc:cc + 256] = cov(fl, target_forms, slice(cc, cc + 256))
            for tj in range(TILE // 256):
                cols = slice(256 * tj, 256 * tj + 256)
                out[slot, :, cols] = out[slot, :, cols] - dot_nt(ph[...], pj[cols, :])
            @pl.when((i - 1) * 8 + row_index == PANELS + col_index)
            def _():
                out[slot] = out[slot] + 0.5 * eye(TILE)
            store(i).start()
        return 0
    lax.fori_loop(0, SLOTS + 1, tile, 0)
    for n in (SLOTS - 1, SLOTS):
        pltpu.make_async_copy(out.at[n % 2], trail_ref.at[n - 1], sems.at[n % 2]).wait()


def exchange_kernel(send_ref, o_ref, buf, send_sem, recv_sem):
    me = lax.axis_index("row")
    count = buf.shape[0]
    other = lambda d: {"row": lax.rem(me + d, count)}
    barrier = pltpu.get_barrier_semaphore()
    for d in range(1, count):
        pl.semaphore_signal(barrier, inc=1, device_id=other(d), device_id_type=pl.DeviceIdType.MESH)
    pl.semaphore_wait(barrier, count - 1)

    def copy(d, place):
        return pltpu.make_async_remote_copy(
            src_ref=send_ref, dst_ref=buf.at[place], send_sem=send_sem.at[d - 1], recv_sem=recv_sem.at[d - 1],
            device_id=other(d), device_id_type=pl.DeviceIdType.MESH)
    for d in range(1, count):
        copy(d, me).start()
    buf[me] = send_ref[...]
    for d in range(1, count):
        copy(d, lax.rem(me + count - d, count)).wait_recv()
    for d in range(1, count):
        copy(d, me).wait_send()
    o_ref[...] = buf[...]


def exchange(send, count):
    vm = pl.BlockSpec(memory_space=pltpu.VMEM)
    shape = (count,) + send.shape
    return pl.pallas_call(
        exchange_kernel,
        out_shape=jax.ShapeDtypeStruct(shape, send.dtype),
        in_specs=[vm],
        out_specs=vm,
        scratch_shapes=[pltpu.VMEM(shape, send.dtype), pltpu.SemaphoreType.DMA((count - 1,)), pltpu.SemaphoreType.DMA((count - 1,))],
        compiler_params=pltpu.CompilerParams(collective_id=0, has_side_effects=True),
        name="exchange",
    )(send)


def main(points, kinds, sites, forms):
    vm = pl.BlockSpec(memory_space=pltpu.VMEM)
    scratch = [
        pltpu.VMEM((3584 + LEAD, 16), bf16),
        pltpu.VMEM((6, 16, LEAD), bf16),
        pltpu.VMEM((6, 16, TILE), bf16),
        pltpu.VMEM((LEAD, LEAD + 2 * BLK), f32),
        pltpu.VMEM((LEAD + 2 * BLK, 2 * BLK), bf16),
        pltpu.VMEM((BLK, BLK), f32),
        pltpu.VMEM((BLK, BLK), f32),
        pltpu.VMEM((BLK, 3 * BLK), bf16),
        pltpu.VMEM((LEAD, LEAD), bf16),
        pltpu.VMEM((LEAD, LEAD), bf16),
        pltpu.VMEM((7 * TILE, LEAD), bf16),
        pltpu.VMEM((7 * TILE, LEAD), bf16),
        pltpu.VMEM((TILE, 256), f32),
        pltpu.VMEM((TILE, LEAD), bf16),
        pltpu.VMEM((TILE, LEAD), bf16),
        pltpu.VMEM((2, TILE, TILE), f32),
        pltpu.SemaphoreType.DMA((2,)),
    ]
    return pl.pallas_call(
        main_kernel,
        out_shape=(jax.ShapeDtypeStruct((SLOTS, 16, LEAD), f32), jax.ShapeDtypeStruct((SLOTS, TILE, TILE), f32)),
        in_specs=[vm] * 4,
        out_specs=(vm, pl.BlockSpec(memory_space=pl.ANY)),
        scratch_shapes=scratch,
        compiler_params=pltpu.CompilerParams(vmem_limit_bytes=60 << 20),
        name="panels",
    )(points, kinds, sites, forms)


def local(grid_points, variable):
    count = lax.axis_size("row")
    place = (PANELS + lax.axis_index("col")) // count
    second = lax.dynamic_index_in_dim(grid_points, place, 1, False)
    kind = lax.dynamic_index_in_dim(variable, place, 0, True)
    send = jnp.concatenate([grid_points[:, 0], variable[:1], second, kind, jnp.zeros((2, TILE), i32)], 0)
    return main(grid_points, variable, exchange(send, count), jnp.asarray(tables()))


def solution(mesh):
    return jax.shard_map(
        local,
        mesh=mesh,
        in_specs=(P(None, None, "row"), P(None, "row")),
        out_specs=(P(None, ("row", "col"), None), P(None, "row", "col")),
        check_vma=False,
    )
```
